32 devices in a mesh: groups: 2 (over y), seq: 4 (over z), proj: 2 (over x), chan: 2 (over core).
Axes of the slice: x: 2, y: 2, z: 4, core: 2. Of those that a mesh axis runs over, the one named last changes fastest.
Arguments:
- tokens: bfloat16 [8192, 8192], P('seq', ('proj', 'chan')), may hold values from -6 to 6
- w_proj: bfloat16 [8192, 3, 512], P('proj', None, ('groups', 'chan')), parts along dimension 2, may hold values from -0.0625 to 0.0625
- short_taps: float32 [3, 3, 512], P(None, None, ('groups', 'chan')), parts along dimension 2, may hold values from -3 to 3
- long_filter: bfloat16 [8192, 512], P(('seq', 'proj'), ('groups', 'chan')), parts along dimension 1, may hold values from -0.0625 to 0.0625
- filter_bias: float32 [512], P(('groups', 'chan')), parts along dimension 0, may hold values from -1 to 1
Outputs:
- mixed: bfloat16 [8192, 512], P(('seq', 'proj'), ('groups', 'chan')), parts along dimension 1
The draws below stay inside these ranges and needn't reach their ends.
There are 2 independent parts, one for each index of `groups`. The reference program is written for one: setup_inputs(seed, part) draws one part's arguments, and reference() takes and returns one part's arrays. A program takes and returns all parts, laid end to end along the dimension named above; an argument that names none is the same for every part. Nothing has to cross between parts.
All inputs are finite; a program needn't handle non-finite values.
Results may differ from the reference program's by a relative error of at most 0.0075.
Values may be sent and summed in bfloat16 or wider, within the bound.
No kernel may reach another device: no remote copies, remote signals or barrier semaphores. Data moves between devices by JAX's collectives and lax.ppermute only.
A program may use at most 128 MiB of HBM per device.

```python
import jax
import jax.numpy as jnp
from jax import lax

D = 8192
C = 256
TAPS = 3
SEQ_LEN = 8192


def block_scale(stream_key, extent, split, low, high):
    loudness = 1.0
    for dim, parts in split:
        heights = jax.random.uniform(jax.random.fold_in(jax.random.fold_in(stream_key, 6), dim), (parts,), jnp.float32, low / len(split), high / len(split))
        loudness = loudness * jnp.repeat(jnp.exp(heights), extent[dim] // parts).reshape((-1,) + (1,) * (len(extent) - 1 - dim))
    return loudness


def gaussian(rng, dims, deviation, limit, pieces=(), held_as=jnp.bfloat16):
    entries = jax.random.normal(rng, dims, jnp.float32) * deviation
    if len(pieces) > 0:
        entries = block_scale(rng, dims, pieces, -0.22, 0.18) * entries
    return jnp.clip(entries, min=-limit, max=limit).astype(held_as)


def setup_inputs(seed: int = 0, part: int = 0) -> dict:
    key_of = jax.random.split(jax.random.key(seed), 6)
    own_keys = jax.random.split(jax.random.fold_in(key_of[5], part), 6)
    return {
        "tokens": gaussian(key_of[0], (SEQ_LEN, D), 1.0, 6.0, ((0, 4), (1, 4))),
        "w_proj": gaussian(own_keys[1], (D, 3, C), D ** -0.5, 0.0625, ((0, 2), (2, 2))),
        "short_taps": gaussian(own_keys[2], (TAPS, 3, C), 0.6, 3.0, ((2, 2),), jnp.float32),
        "long_filter": gaussian(own_keys[3], (SEQ_LEN, C), SEQ_LEN ** -0.5, 0.0625, ((0, 8), (1, 2))),
        "filter_bias": jnp.clip(jax.random.uniform(own_keys[4], (C,), jnp.float32, -1.0, 1.0) * block_scale(own_keys[4], (C,), ((0, 2),), -0.4, 0.0), -1.0, 1.0),
    }


def reference(tokens, w_proj, short_taps, long_filter, filter_bias):
    projected = jnp.dot(tokens, w_proj.reshape(D, 3 * C), preferred_element_type=jnp.float32)
    taps_flat = short_taps.reshape(TAPS, 3 * C)
    featured = taps_flat[0] * projected
    for shift_by in range(1, TAPS):
        delayed = jnp.concatenate([jnp.zeros((shift_by, 3 * C), projected.dtype), projected[:-shift_by]], axis=0)
        featured = featured + taps_flat[shift_by] * delayed
    query_part = featured[:, :C]
    gated_low = (featured[:, C:2 * C] * featured[:, 2 * C:]).astype(jnp.bfloat16)
    gated_low = lax.optimization_barrier(gated_low)
    gated_rows = gated_low.astype(jnp.float32)
    filter_rows = long_filter.astype(jnp.float32)
    spectrum = jnp.fft.rfft(gated_rows, n=2 * SEQ_LEN, axis=0) * jnp.fft.rfft(filter_rows, n=2 * SEQ_LEN, axis=0)
    long_conv = jnp.fft.irfft(spectrum, n=2 * SEQ_LEN, axis=0)[:SEQ_LEN]
    return (query_part * (long_conv + filter_bias * gated_rows)).astype(jnp.bfloat16)
```

```python
import functools

import jax
import jax.numpy as jnp
from jax import lax
from jax.experimental import pallas as pl
from jax.experimental.pallas import tpu as pltpu
from jax.sharding import PartitionSpec as P

LANES = 128
HALO = 16
GROUP = 8
f32 = jnp.float32
bf16 = jnp.bfloat16
RING = ("seq", "proj")


def in_vmem():
    return pl.BlockSpec(memory_space=pltpu.VMEM)


def params(mib):
    return pltpu.CompilerParams(vmem_limit_bytes=mib << 20)


def matmul_body(tok_ref, halo_ref, w_ref, out_ref, *, tile):
    step = pl.program_id(0)
    slabs, _, width = out_ref.shape

    def put(rows, start):
        product = jnp.dot(rows, w_ref[...], preferred_element_type=f32).astype(out_ref.dtype)
        for slab in range(slabs):
            out_ref[slab, pl.ds(start, rows.shape[0]), :] = product[:, slab * width : (slab + 1) * width]

    @pl.when(step == 0)
    def _():
        put(halo_ref[...], 0)

    put(tok_ref[...], pl.multiple_of(HALO + step * tile, HALO))


def matmul(tokens, halo, weights, slabs, dtype):
    rows, depth = tokens.shape
    cols = weights.shape[1]
    tile = min(256, rows)
    out = (slabs, rows + HALO, cols // slabs)
    return pl.pallas_call(
        functools.partial(matmul_body, tile=tile),
        out_shape=jax.ShapeDtypeStruct(out, dtype),
        grid=(rows // tile,),
        in_specs=[
            pl.BlockSpec((tile, depth), lambda i: (i, 0)),
            pl.BlockSpec((HALO, depth), lambda i: (0, 0)),
            pl.BlockSpec((depth, cols), lambda i: (0, 0)),
        ],
        out_specs=pl.BlockSpec(out, lambda i: (0, 0, 0)),
        compiler_params=params(40),
        name="project",
    )(tokens, halo, weights)


def filter_body(h_ref, out_ref, *, order):
    dests, blocks, chans, _ = out_ref.shape
    for block in range(blocks):
        turned = h_ref[block * LANES : (block + 1) * LANES, :].astype(f32).T.astype(bf16)
        for dest in range(dests):
            first = order[dest]
            out_ref[dest, block] = turned[first : first + chans]


def filter_blocks(long_filter, order, chans):
    rows = long_filter.shape[0]
    return pl.pallas_call(
        functools.partial(filter_body, order=order),
        out_shape=jax.ShapeDtypeStruct((len(order), rows // LANES, chans, LANES), bf16),
        in_specs=[in_vmem()],
        out_specs=in_vmem(),
        compiler_params=params(32),
        name="filter_blocks",
    )(long_filter)


def short_conv(padded, taps, start, size):
    total = taps[0:1] * padded[start : start + size, :]
    for lag in range(1, taps.shape[0]):
        total = total + taps[lag : lag + 1] * padded[start - lag : start - lag + size, :]
    return total


def gate_body(kept_ref, got_ref, taps_ref, out_ref, whole):
    dests, blocks, chans, _ = out_ref.shape
    half = dests * chans
    total = kept_ref[...]
    for part in range(got_ref.shape[0]):
        total = total + got_ref[part].astype(f32)
    whole[...] = total
    taps = taps_ref[...]
    for block in range(blocks):
        mixed = short_conv(whole, taps, HALO + block * LANES, LANES).T
        gated = (mixed[:half] * mixed[half:]).astype(bf16)
        for dest in range(dests):
            out_ref[dest, block] = gated[dest * chans : (dest + 1) * chans]


def gate(kept, got, taps, dests):
    rows, width = kept.shape
    blocks = (rows - HALO) // LANES
    return pl.pallas_call(
        gate_body,
        out_shape=jax.ShapeDtypeStruct((dests, blocks, width // 2 // dests, LANES), bf16),
        in_specs=[in_vmem()] * 3,
        out_specs=in_vmem(),
        scratch_shapes=[pltpu.VMEM((rows, width), f32)],
        compiler_params=params(32),
        name="gate",
    )(kept, got, taps)


def conv_body(g_ref, h_ref, bias_ref, out_ref, gs, hs, acc, padded, lhs, toep, *, chans, blocks):
    gs[...] = g_ref[...].astype(f32)
    hs[...] = h_ref[...].astype(f32)
    row = lax.broadcasted_iota(jnp.int32, (LANES, LANES), 0)
    col = lax.broadcasted_iota(jnp.int32, (LANES, LANES), 1)
    keep = col >= row
    padded[0:GROUP, :] = jnp.zeros((GROUP, LANES), f32)
    padded[blocks + GROUP : blocks + 2 * GROUP, :] = jnp.zeros((GROUP, LANES), f32)
    steps = blocks // GROUP

    def channel(c, _):
        series = gs[pl.ds(c, blocks, stride=chans), :]
        padded[GROUP : GROUP + blocks, :] = series
        for r in range(GROUP):
            lhs[:, r * LANES : (r + 1) * LANES] = padded[
                GROUP - r : GROUP - r + blocks + GROUP, :
            ].astype(bf16)
        acc[...] = jnp.zeros_like(acc)

        def build(step, slot, before):
            for r in range(GROUP):
                taps = hs[pl.ds((step * GROUP + r) * chans + c, 1), :]
                turned = pltpu.roll(
                    jnp.broadcast_to(taps, (LANES, LANES)), 0, 1, stride=1, stride_axis=0
                )
                toep[slot, r * LANES : (r + 1) * LANES, :] = jnp.where(keep, turned, before).astype(bf16)
                before = turned
            return before

        before = jnp.zeros((LANES, LANES), f32)
        if steps <= 8:
            for step in range(steps):
                before = build(step, step % 2, before)
                size = min(blocks + GROUP, blocks - step * GROUP)
                acc[step * GROUP : step * GROUP + size, :] += jnp.dot(
                    lhs[0:size, :], toep[step % 2], preferred_element_type=f32
                )
        else:

            def one(step, before):
                before = build(step, 0, before)
                rows = pl.ds(pl.multiple_of(step * GROUP, GROUP), blocks + GROUP)
                acc[rows, :] += jnp.dot(lhs[...], toep[0], preferred_element_type=f32)
                return before

            lax.fori_loop(0, steps, one, before)
        gs[pl.ds(c, blocks, stride=chans), :] = acc[0:blocks, :] + bias_ref[0, c] * series
        return 0

    lax.fori_loop(0, chans, channel, 0)
    out_ref[...] = gs[...].astype(bf16)


def long_conv(gated, filt, bias, chans):
    rows = gated.shape[0]
    blocks = rows // chans
    return pl.pallas_call(
        functools.partial(conv_body, chans=chans, blocks=blocks),
        out_shape=jax.ShapeDtypeStruct((rows, LANES), bf16),
        in_specs=[in_vmem(), in_vmem(), pl.BlockSpec(memory_space=pltpu.SMEM)],
        out_specs=in_vmem(),
        scratch_shapes=[
            pltpu.VMEM((rows, LANES), f32),
            pltpu.VMEM((rows, LANES), f32),
            pltpu.VMEM((2 * blocks + GROUP, LANES), f32),
            pltpu.VMEM((blocks + 2 * GROUP, LANES), f32),
            pltpu.VMEM((blocks + GROUP, GROUP * LANES), bf16),
            pltpu.VMEM((2, GROUP * LANES, LANES), bf16),
        ],
        compiler_params=params(48),
        name="long_conv",
    )(gated, filt, bias)


def finish_body(kept_ref, got_ref, taps_ref, z_ref, out_ref, whole, *, order):
    total = kept_ref[...]
    for part in range(got_ref.shape[0]):
        total = total + got_ref[part].astype(f32)
    whole[...] = total
    taps = taps_ref[...]
    sources = sorted(range(len(order)), key=lambda i: order[i])
    for block in range(z_ref.shape[1]):
        z = jnp.concatenate([z_ref[i, block].astype(f32) for i in sources], axis=0)
        query = short_conv(whole, taps, HALO + block * LANES, LANES)
        out_ref[block * LANES : (block + 1) * LANES, :] = (query * z.T).astype(bf16)


def finish(kept, got, taps, z, order):
    rows, width = kept.shape
    return pl.pallas_call(
        functools.partial(finish_body, order=order),
        out_shape=jax.ShapeDtypeStruct((rows - HALO, width), bf16),
        in_specs=[in_vmem()] * 4,
        out_specs=in_vmem(),
        scratch_shapes=[pltpu.VMEM((rows, width), f32)],
        compiler_params=params(32),
        name="finish",
    )(kept, got, taps, z)


def swap(array, axis, by=1):
    size = lax.axis_size(axis)
    return lax.ppermute(array, axis, [(i, (i + by) % size) for i in range(size)])


def shards(tokens, w_proj, short_taps, long_filter, filter_bias):
    n_proj = lax.axis_size("proj")
    n_seq = lax.axis_size("seq")
    p = lax.axis_index("proj")
    s = lax.axis_index("seq")
    c = lax.axis_index("chan")
    rows, depth = tokens.shape
    own_rows = rows // n_proj
    channels = w_proj.shape[2]
    slab = channels // n_proj
    chans = slab // n_seq
    order = [pp * slab + ss * chans for ss in range(n_seq) for pp in range(n_proj)]

    w = w_proj.transpose(1, 0, 2)

    def by_slab(quarter):
        kv = quarter[1:].reshape(2, depth, n_proj, slab).transpose(1, 2, 0, 3)
        return kv.reshape(depth, 2 * channels), quarter[0]

    own_kv, own_q = by_slab(lax.dynamic_slice_in_dim(w, c * depth, depth, 1))
    out_kv, out_q = by_slab(lax.dynamic_slice_in_dim(w, (1 - c) * depth, depth, 1))
    other_kv, other_q = swap(out_kv, "chan"), swap(out_q, "chan")
    halo = lax.ppermute(tokens[rows - HALO :], "seq", [(i, i + 1) for i in range(n_seq - 1)])

    filt = filter_blocks(long_filter, order, chans)
    filt = lax.all_to_all(filt, RING, split_axis=0, concat_axis=0, tiled=True)

    away = swap(matmul(tokens, halo, other_kv, n_proj, bf16), "chan")
    chip = matmul(tokens, halo, own_kv, n_proj, f32) + away.astype(f32)
    kept = lax.dynamic_index_in_dim(chip, p, 0, keepdims=False)
    got = jnp.stack(
        [
            swap(lax.dynamic_index_in_dim(chip, (p + by) % n_proj, 0, keepdims=False).astype(bf16), "proj", by)
            for by in range(1, n_proj)
        ]
    )

    away_q = swap(matmul(tokens, halo, other_q, 1, bf16), "chan")[0]
    chip_q = matmul(tokens, halo, own_q, 1, f32)[0] + away_q.astype(f32)
    kept_q = lax.dynamic_slice_in_dim(chip_q, p * own_rows, own_rows + HALO, 0)
    got_q = jnp.stack(
        [
            swap(
                lax.dynamic_slice_in_dim(
                    chip_q, ((p + by) % n_proj) * own_rows, own_rows + HALO, 0
                ).astype(bf16),
                "proj",
                by,
            )
            for by in range(1, n_proj)
        ]
    )

    taps_kv = lax.dynamic_slice_in_dim(short_taps[:, 1:], p * slab, slab, 2).reshape(-1, 2 * slab)
    gated = gate(kept, got, taps_kv, n_seq)
    gated = lax.all_to_all(gated, "seq", split_axis=0, concat_axis=0, tiled=True)
    bias = lax.dynamic_slice_in_dim(filter_bias, p * slab + s * chans, chans, 0)[None]
    z = long_conv(gated.reshape(-1, LANES), filt.reshape(-1, LANES), bias, chans)
    z = z.reshape(n_seq * n_proj, -1, chans, LANES)
    z = lax.all_to_all(z, RING, split_axis=0, concat_axis=0, tiled=True)
    return finish(kept_q, got_q, short_taps[:, 0], z, order)


def solution(mesh):
    placed = (
        P("seq", ("proj", "chan")),
        P("proj", None, ("groups", "chan")),
        P(None, None, ("groups", "chan")),
        P(("seq", "proj"), ("groups", "chan")),
        P(("groups", "chan")),
    )
    return jax.shard_map(
        shards,
        mesh=mesh,
        in_specs=placed,
        out_specs=P(("seq", "proj"), ("groups", "chan")),
        check_vma=False,
    )
```

```python
import functools
import math

import jax
import jax.numpy as jnp
from jax import lax
from jax.experimental import pallas as pl
from jax.experimental.pallas import tpu as pltpu
from jax.sharding import PartitionSpec as P

LANES = 128
HALO = 16
GROUP = 8
TILE = 256
BRIEF = pl.CostEstimate(flops=1, transcendentals=0, bytes_accessed=1)
f32 = jnp.float32
bf16 = jnp.bfloat16
RING = ("seq", "proj")


def in_vmem():
    return pl.BlockSpec(memory_space=pltpu.VMEM)


def params(mib):
    return pltpu.CompilerParams(vmem_limit_bytes=mib << 20)


def spread(out_ref, product, at, width):
    slabs, _, wide = out_ref.shape
    part = width // slabs
    for slab in range(slabs):
        pieces = [
            product[:, j * width + slab * part : j * width + (slab + 1) * part]
            for j in range(wide // part)
        ]
        whole = pieces[0] if len(pieces) == 1 else jnp.concatenate(pieces, axis=1)
        out_ref[slab, at : at + product.shape[0], :] = whole.astype(out_ref.dtype)


def project_body(place_ref, tok_ref, *refs, halo):
    if halo:
        halo_ref, w_ref, other_ref, kv_own, kv_away, q_own, q_away, own_w, query_w, sems = refs
    else:
        w_ref, other_ref, kv_own, kv_away, q_own, q_away, own_w, query_w, sems = refs
    rows, depth = tok_ref.shape
    width = w_ref.shape[2]
    start = place_ref[1] * depth
    targets = [(0, query_w, 0), (1, own_w, 0), (2, own_w, width)]
    copies = [
        pltpu.make_async_copy(
            w_ref.at[pick, pl.ds(start, depth), :], target.at[:, pl.ds(at, width)], sems.at[pick]
        )
        for pick, target, at in targets
    ]
    for copy in copies:
        copy.start()
    tile = min(TILE, rows)

    def passes(weights, put):
        if halo:
            put(jnp.dot(halo_ref[...], weights, preferred_element_type=f32), 0)
        for at in range(0, rows, tile):
            product = jnp.dot(tok_ref[at : at + tile, :], weights, preferred_element_type=f32)
            put(product, (HALO if halo else 0) + at)

    def put_query(product, at):
        q_own[at : at + product.shape[0], :] = product[:, :width]
        q_away[at : at + product.shape[0], :] = product[:, width:].astype(bf16)

    passes(other_ref[:, : 2 * width], lambda product, at: spread(kv_away, product, at, width))
    query_w[:, width:] = other_ref[:, 2 * width :]
    for copy in copies:
        copy.wait()
    passes(own_w[...], lambda product, at: spread(kv_own, product, at, width))
    passes(query_w[...], put_query)


def project(place, tokens, halo, w, other, slabs):
    rows, depth = tokens.shape
    width = w.shape[2]
    count = rows + (0 if halo is None else HALO)
    keys = (slabs, count, 2 * width // slabs)
    extra = [] if halo is None else [halo]
    return pl.pallas_call(
        functools.partial(project_body, halo=halo is not None),
        out_shape=(
            jax.ShapeDtypeStruct(keys, f32),
            jax.ShapeDtypeStruct(keys, bf16),
            jax.ShapeDtypeStruct((count, width), f32),
            jax.ShapeDtypeStruct((count, width), bf16),
        ),
        in_specs=[pl.BlockSpec(memory_space=pltpu.SMEM)]
        + [in_vmem()] * (1 + len(extra))
        + [pl.BlockSpec(memory_space=pl.ANY), in_vmem()],
        out_specs=(in_vmem(),) * 4,
        scratch_shapes=[
            pltpu.VMEM((depth, 2 * width), bf16),
            pltpu.VMEM((depth, 2 * width), bf16),
            pltpu.SemaphoreType.DMA((3,)),
        ],
        compiler_params=params(14),
        cost_estimate=BRIEF,
        name="project",
    )(place, tokens, *extra, w, other)


def mix_body(place_ref, own_a, came_a, own_b, came_b, kept_ref, send_ref):
    slabs, rows = own_a.shape[:2]
    p = place_ref[0]

    def put(slab, store):
        last = own_b[slab] + came_b[slab].astype(f32)
        store(pl.ds(0, HALO), last[:HALO])
        store(pl.ds(HALO, rows), own_a[slab] + came_a[slab].astype(f32))
        store(pl.ds(HALO + rows, last.shape[0] - HALO), last[HALO:])

    def keep(at, value):
        kept_ref[at, :] = value

    put(p, keep)
    for by in range(1, slabs):

        def send(at, value):
            send_ref[by - 1, at, :] = value.astype(bf16)

        put(lax.rem(p + by, slabs), send)


def mix(place, own_a, came_a, own_b, came_b):
    slabs, rows, width = own_a.shape
    rows += own_b.shape[1]
    return pl.pallas_call(
        mix_body,
        out_shape=(
            jax.ShapeDtypeStruct((rows, width), f32),
            jax.ShapeDtypeStruct((slabs - 1, rows, width), bf16),
        ),
        in_specs=[pl.BlockSpec(memory_space=pltpu.SMEM)] + [in_vmem()] * 4,
        out_specs=(in_vmem(), in_vmem()),
        compiler_params=params(8),
        cost_estimate=BRIEF,
        name="mix",
    )(place, own_a, came_a, own_b, came_b)


def mix_rows_body(place_ref, own_a, came_a, own_b, came_b, kept_ref, send_ref, whole):
    parts = send_ref.shape[0] + 1
    count = kept_ref.shape[0]
    step = count - HALO
    rows = own_a.shape[0]
    p = place_ref[0]
    last = own_b[...] + came_b[...].astype(f32)
    whole[0:HALO, :] = last[:HALO]
    whole[HALO : HALO + rows, :] = own_a[...] + came_a[...].astype(f32)
    whole[HALO + rows :, :] = last[HALO:]

    def part(i):
        return whole[pl.ds(pl.multiple_of(i * step, HALO), count), :]

    kept_ref[...] = part(p)
    for by in range(1, parts):
        send_ref[by - 1] = part(lax.rem(p + by, parts)).astype(bf16)


def mix_rows(place, own_a, came_a, own_b, came_b, parts):
    rows, width = own_a.shape
    rows += own_b.shape[0]
    count = (rows - HALO) // parts + HALO
    return pl.pallas_call(
        mix_rows_body,
        out_shape=(
            jax.ShapeDtypeStruct((count, width), f32),
            jax.ShapeDtypeStruct((parts - 1, count, width), bf16),
        ),
        in_specs=[pl.BlockSpec(memory_space=pltpu.SMEM)] + [in_vmem()] * 4,
        out_specs=(in_vmem(), in_vmem()),
        scratch_shapes=[pltpu.VMEM((rows, width), f32)],
        compiler_params=params(8),
        cost_estimate=BRIEF,
        name="mix_rows",
    )(place, own_a, came_a, own_b, came_b)


def filter_body(h_ref, out_ref, *, order):
    dests, blocks, chans, _ = out_ref.shape
    for block in range(blocks):
        turned = h_ref[block * LANES : (block + 1) * LANES, :].astype(f32).T.astype(bf16)
        for dest in range(dests):
            first = order[dest]
            out_ref[dest, block] = turned[first : first + chans]


def filter_blocks(long_filter, order, chans):
    rows = long_filter.shape[0]
    return pl.pallas_call(
        functools.partial(filter_body, order=order),
        out_shape=jax.ShapeDtypeStruct((len(order), rows // LANES, chans, LANES), bf16),
        in_specs=[in_vmem()],
        out_specs=in_vmem(),
        compiler_params=params(32),
        cost_estimate=BRIEF,
        name="filter_blocks",
    )(long_filter)


def short_conv(padded, taps, start, size):
    total = taps[0:1] * padded[start : start + size, :]
    for lag in range(1, taps.shape[0]):
        total = total + taps[lag : lag + 1] * padded[start - lag : start - lag + size, :]
    return total


def gate_body(kept_ref, got_ref, taps_ref, out_ref, whole):
    dests, blocks, chans, _ = out_ref.shape
    half = dests * chans
    total = kept_ref[...]
    for part in range(got_ref.shape[0]):
        total = total + got_ref[part].astype(f32)
    whole[...] = total
    taps = taps_ref[...]
    for block in range(blocks):
        mixed = short_conv(whole, taps, HALO + block * LANES, LANES).T
        gated = (mixed[:half] * mixed[half:]).astype(bf16)
        for dest in range(dests):
            out_ref[dest, block] = gated[dest * chans : (dest + 1) * chans]


def gate(kept, got, taps, dests):
    rows, width = kept.shape
    blocks = (rows - HALO) // LANES
    return pl.pallas_call(
        gate_body,
        out_shape=jax.ShapeDtypeStruct((dests, blocks, width // 2 // dests, LANES), bf16),
        in_specs=[in_vmem()] * 3,
        out_specs=in_vmem(),
        scratch_shapes=[pltpu.VMEM((rows, width), f32)],
        compiler_params=params(12),
        cost_estimate=BRIEF,
        name="gate",
    )(kept, got, taps)


def conv_body(g_ref, h_ref, bias_ref, out_ref, gs, hs, *scratch, chans, blocks):
    gs[...] = g_ref[...].astype(f32)
    hs[...] = h_ref[...].astype(f32)
    row = lax.broadcasted_iota(jnp.int32, (LANES, LANES), 0)
    col = lax.broadcasted_iota(jnp.int32, (LANES, LANES), 1)
    keep = col >= row
    steps = blocks // GROUP
    sets = [scratch[i : i + 4] for i in range(0, len(scratch), 4)]
    for acc, padded, lhs, toep in sets:
        padded[0:GROUP, :] = jnp.zeros((GROUP, LANES), f32)
        padded[blocks + GROUP : blocks + 2 * GROUP, :] = jnp.zeros((GROUP, LANES), f32)

    def channels(first, _):
        every = [first + i * (chans // len(sets)) for i in range(len(sets))]
        series = []
        for c, (acc, padded, lhs, toep) in zip(every, sets):
            series.append(gs[pl.ds(c, blocks, stride=chans), :])
            padded[GROUP : GROUP + blocks, :] = series[-1]
            for r in range(GROUP):
                lhs[:, r * LANES : (r + 1) * LANES] = padded[
                    GROUP - r : GROUP - r + blocks + GROUP, :
                ].astype(bf16)
            acc[...] = jnp.zeros_like(acc)

        def build(c, step, target, before):
            for r in range(GROUP):
                taps = hs[pl.ds((step * GROUP + r) * chans + c, 1), :].astype(bf16)
                turned = pltpu.roll(
                    jnp.broadcast_to(taps, (LANES, LANES)), 0, 1, stride=1, stride_axis=0
                )
                target[r * LANES : (r + 1) * LANES, :] = jnp.where(keep, turned, before)
                before = turned
            return before

        none = jnp.zeros((LANES, LANES), bf16)
        if steps <= 8:
            before = [none] * len(sets)
            for step in range(steps):
                size = min(blocks + GROUP, blocks - step * GROUP)
                for i, (c, (acc, padded, lhs, toep)) in enumerate(zip(every, sets)):
                    target = toep.at[step % 2]
                    before[i] = build(c, step, target, before[i])
                    acc[step * GROUP : step * GROUP + size, :] += jnp.dot(
                        lhs[0:size, :], target[...], preferred_element_type=f32
                    )
        else:
            for c, (acc, padded, lhs, toep) in zip(every, sets):

                def one(step, before):
                    before = build(c, step, toep.at[0], before)
                    rows = pl.ds(pl.multiple_of(step * GROUP, GROUP), blocks + GROUP)
                    acc[rows, :] += jnp.dot(lhs[...], toep[0], preferred_element_type=f32)
                    return before

                lax.fori_loop(0, steps, one, none)
        for c, own, (acc, padded, lhs, toep) in zip(every, series, sets):
            gs[pl.ds(c, blocks, stride=chans), :] = acc[0:blocks, :] + bias_ref[0, c] * own
        return 0

    lax.fori_loop(0, chans // len(sets), channels, 0)
    out_ref[...] = gs[...].astype(bf16)


def long_conv(gated, filt, bias, chans):
    rows = gated.shape[0]
    blocks = rows // chans
    together = math.gcd(chans, 4)
    one = [
        pltpu.VMEM((2 * blocks + GROUP, LANES), f32),
        pltpu.VMEM((blocks + 2 * GROUP, LANES), f32),
        pltpu.VMEM((blocks + GROUP, GROUP * LANES), bf16),
        pltpu.VMEM((2, GROUP * LANES, LANES), bf16),
    ]
    return pl.pallas_call(
        functools.partial(conv_body, chans=chans, blocks=blocks),
        out_shape=jax.ShapeDtypeStruct((rows, LANES), bf16),
        in_specs=[in_vmem(), in_vmem(), pl.BlockSpec(memory_space=pltpu.SMEM)],
        out_specs=in_vmem(),
        scratch_shapes=[pltpu.VMEM((rows, LANES), f32), pltpu.VMEM((rows, LANES), f32)] + one * together,
        compiler_params=params(24),
        cost_estimate=BRIEF,
        name="long_conv",
    )(gated, filt, bias)


def finish_body(kept_ref, got_ref, taps_ref, z_ref, out_ref, whole, *, order):
    total = kept_ref[...]
    for part in range(got_ref.shape[0]):
        total = total + got_ref[part].astype(f32)
    whole[...] = total
    taps = taps_ref[...]
    sources = sorted(range(len(order)), key=lambda i: order[i])
    for block in range(z_ref.shape[1]):
        z = jnp.concatenate([z_ref[i, block].astype(f32) for i in sources], axis=0)
        query = short_conv(whole, taps, HALO + block * LANES, LANES)
        out_ref[block * LANES : (block + 1) * LANES, :] = (query * z.T).astype(bf16)


def finish(kept, got, taps, z, order):
    rows, width = kept.shape
    return pl.pallas_call(
        functools.partial(finish_body, order=order),
        out_shape=jax.ShapeDtypeStruct((rows - HALO, width), bf16),
        in_specs=[in_vmem()] * 4,
        out_specs=in_vmem(),
        scratch_shapes=[pltpu.VMEM((rows, width), f32)],
        compiler_params=params(32),
        cost_estimate=BRIEF,
        name="finish",
    )(kept, got, taps, z)


def swap(array, axis, by=1):
    size = lax.axis_size(axis)
    return lax.ppermute(array, axis, [(i, (i + by) % size) for i in range(size)])


def shards(tokens, w_proj, short_taps, long_filter, filter_bias):
    n_proj = lax.axis_size("proj")
    n_seq = lax.axis_size("seq")
    p = lax.axis_index("proj")
    s = lax.axis_index("seq")
    c = lax.axis_index("chan")
    rows, depth = tokens.shape
    own_rows = rows // n_proj
    channels = w_proj.shape[2]
    slab = channels // n_proj
    chans = slab // n_seq
    order = [pp * slab + ss * chans for ss in range(n_seq) for pp in range(n_proj)]

    place = jnp.stack([p, c]).astype(jnp.int32)
    barrier = lax.optimization_barrier

    def exchange(send):
        return jnp.stack([swap(send[by - 1], "proj", by) for by in range(1, n_proj)])

    w = w_proj.transpose(1, 0, 2)
    w_hbm = pltpu.with_memory_space_constraint(w, pltpu.HBM)
    theirs = [
        lax.dynamic_slice(w, (pick, (1 - c) * depth, 0), (1, depth, channels))[0]
        for pick in (1, 2, 0)
    ]
    other = swap(jnp.concatenate(theirs, axis=1), "chan")
    halo = lax.ppermute(tokens[rows - HALO :], "seq", [(i, i + 1) for i in range(n_seq - 1)])

    half = rows // 2
    own_a, away_a, own_qa, away_qa = project(place, tokens[:half], None, w_hbm, other, n_proj)
    came_a = swap(away_a, "chan")
    halo, away_qa = barrier((halo, away_qa))
    own_b, away_b, own_qb, away_qb = project(place, tokens[half:], halo, w_hbm, other, n_proj)
    came_b = swap(away_b, "chan")

    kept, send = mix(place, own_a, came_a, own_b, came_b)
    got = exchange(send)

    long_filter, away_qa, away_qb, send = barrier((long_filter, away_qa, away_qb, send))
    filt = filter_blocks(long_filter, order, chans)
    filt = lax.all_to_all(filt, RING, split_axis=0, concat_axis=0, tiled=True)

    kept_q, send_q = mix_rows(place, own_qa, swap(away_qa, "chan"), own_qb, swap(away_qb, "chan"), n_proj)
    got, filt, send_q = barrier((got, filt, send_q))
    got_q = exchange(send_q)

    taps_kv = lax.dynamic_slice_in_dim(short_taps[:, 1:], p * slab, slab, 2).reshape(-1, 2 * slab)
    gated = gate(kept, got, taps_kv, n_seq)
    gated = lax.all_to_all(gated, "seq", split_axis=0, concat_axis=0, tiled=True)
    gated, got_q = barrier((gated, got_q))
    bias = lax.dynamic_slice_in_dim(filter_bias, p * slab + s * chans, chans, 0)[None]
    z = long_conv(gated.reshape(-1, LANES), filt.reshape(-1, LANES), bias, chans)
    z = z.reshape(n_seq * n_proj, -1, chans, LANES)
    z = lax.all_to_all(z, RING, split_axis=0, concat_axis=0, tiled=True)
    return finish(kept_q, got_q, short_taps[:, 0], z, order)


def solution(mesh):
    placed = (
        P("seq", ("proj", "chan")),
        P("proj", None, ("groups", "chan")),
        P(None, None, ("groups", "chan")),
        P(("seq", "proj"), ("groups", "chan")),
        P(("groups", "chan")),
    )
    return jax.shard_map(
        shards,
        mesh=mesh,
        in_specs=placed,
        out_specs=P(("seq", "proj"), ("groups", "chan")),
        check_vma=False,
    )
```

```python
import functools
import math

import jax
import jax.numpy as jnp
from jax import lax
from jax.experimental import pallas as pl
from jax.experimental.pallas import tpu as pltpu
from jax.sharding import PartitionSpec as P

LANES = 128
HALO = 16
GROUP = 8
TILE = 256
BRIEF = pl.CostEstimate(flops=1, transcendentals=0, bytes_accessed=1)
f32 = jnp.float32
bf16 = jnp.bfloat16
RING = ("seq", "proj")


def in_vmem():
    return pl.BlockSpec(memory_space=pltpu.VMEM)


def params(mib):
    return pltpu.CompilerParams(vmem_limit_bytes=mib << 20)


def spread(out_ref, product, at, width):
    slabs, _, wide = out_ref.shape
    part = width // slabs
    for slab in range(slabs):
        pieces = [
            product[:, j * width + slab * part : j * width + (slab + 1) * part]
            for j in range(wide // part)
        ]
        whole = pieces[0] if len(pieces) == 1 else jnp.concatenate(pieces, axis=1)
        out_ref[slab, at : at + product.shape[0], :] = whole.astype(out_ref.dtype)


def project_body(place_ref, tok_ref, *refs, halo):
    if halo:
        halo_ref, w_ref, other_ref, kv_own, kv_away, q_own, q_away, own_w, other_w, query_w, sems = refs
    else:
        w_ref, other_ref, kv_own, kv_away, q_own, q_away, own_w, other_w, query_w, sems = refs
    rows, depth = tok_ref.shape
    width = w_ref.shape[2]
    start = place_ref[1] * depth
    targets = [(0, query_w, 0), (1, own_w, 0), (2, own_w, width)]
    copies = [
        pltpu.make_async_copy(
            w_ref.at[pick, pl.ds(start, depth), :], target.at[:, pl.ds(at, width)], sems.at[pick]
        )
        for pick, target, at in targets
    ]
    for copy in copies:
        copy.start()
    tile = min(TILE, rows)

    def passes(weights, put):
        if halo:
            put(jnp.dot(halo_ref[...], weights, preferred_element_type=f32), 0)
        for at in range(0, rows, tile):
            product = jnp.dot(tok_ref[at : at + tile, :], weights, preferred_element_type=f32)
            put(product, (HALO if halo else 0) + at)

    def put_query(product, at):
        q_own[at : at + product.shape[0], :] = product[:, :width]
        q_away[at : at + product.shape[0], :] = product[:, width:].astype(bf16)

    other_w[:, :width] = other_ref[1]
    other_w[:, width:] = other_ref[2]
    passes(other_w[...], lambda product, at: spread(kv_away, product, at, width))
    query_w[:, width:] = other_ref[0]
    for copy in copies:
        copy.wait()
    passes(own_w[...], lambda product, at: spread(kv_own, product, at, width))
    passes(query_w[...], put_query)


def project(place, tokens, halo, w, other, slabs):
    rows, depth = tokens.shape
    width = w.shape[2]
    count = rows + (0 if halo is None else HALO)
    keys = (slabs, count, 2 * width // slabs)
    extra = [] if halo is None else [halo]
    return pl.pallas_call(
        functools.partial(project_body, halo=halo is not None),
        out_shape=(
            jax.ShapeDtypeStruct(keys, f32),
            jax.ShapeDtypeStruct(keys, bf16),
            jax.ShapeDtypeStruct((count, width), f32),
            jax.ShapeDtypeStruct((count, width), bf16),
        ),
        in_specs=[pl.BlockSpec(memory_space=pltpu.SMEM)]
        + [in_vmem()] * (1 + len(extra))
        + [pl.BlockSpec(memory_space=pl.ANY), in_vmem()],
        out_specs=(in_vmem(),) * 4,
        scratch_shapes=[
            pltpu.VMEM((depth, 2 * width), bf16),
            pltpu.VMEM((depth, 2 * width), bf16),
            pltpu.VMEM((depth, 2 * width), bf16),
            pltpu.SemaphoreType.DMA((3,)),
        ],
        compiler_params=params(14),
        cost_estimate=BRIEF,
        name="project",
    )(place, tokens, *extra, w, other)


def mix_body(place_ref, own_a, came_a, own_b, came_b, kept_ref, send_ref):
    slabs, rows = own_a.shape[:2]
    p = place_ref[0]

    def put(slab, store):
        last = own_b[slab] + came_b[slab].astype(f32)
        store(pl.ds(0, HALO), last[:HALO])
        store(pl.ds(HALO, rows), own_a[slab] + came_a[slab].astype(f32))
        store(pl.ds(HALO + rows, last.shape[0] - HALO), last[HALO:])

    def keep(at, value):
        kept_ref[at, :] = value

    put(p, keep)
    for by in range(1, slabs):

        def send(at, value):
            send_ref[by - 1, at, :] = value.astype(bf16)

        put(lax.rem(p + by, slabs), send)


def mix(place, own_a, came_a, own_b, came_b):
    slabs, rows, width = own_a.shape
    rows += own_b.shape[1]
    return pl.pallas_call(
        mix_body,
        out_shape=(
            jax.ShapeDtypeStruct((rows, width), f32),
            jax.ShapeDtypeStruct((slabs - 1, rows, width), bf16),
        ),
        in_specs=[pl.BlockSpec(memory_space=pltpu.SMEM)] + [in_vmem()] * 4,
        out_specs=(in_vmem(), in_vmem()),
        compiler_params=params(8),
        cost_estimate=BRIEF,
        name="mix",
    )(place, own_a, came_a, own_b, came_b)


def mix_rows_body(place_ref, own_a, came_a, own_b, came_b, kept_ref, send_ref, whole):
    parts = send_ref.shape[0] + 1
    count = kept_ref.shape[0]
    step = count - HALO
    rows = own_a.shape[0]
    p = place_ref[0]
    last = own_b[...] + came_b[...].astype(f32)
    whole[0:HALO, :] = last[:HALO]
    whole[HALO : HALO + rows, :] = own_a[...] + came_a[...].astype(f32)
    whole[HALO + rows :, :] = last[HALO:]

    def part(i):
        return whole[pl.ds(pl.multiple_of(i * step, HALO), count), :]

    kept_ref[...] = part(p)
    for by in range(1, parts):
        send_ref[by - 1] = part(lax.rem(p + by, parts)).astype(bf16)


def mix_rows(place, own_a, came_a, own_b, came_b, parts):
    rows, width = own_a.shape
    rows += own_b.shape[0]
    count = (rows - HALO) // parts + HALO
    return pl.pallas_call(
        mix_rows_body,
        out_shape=(
            jax.ShapeDtypeStruct((count, width), f32),
            jax.ShapeDtypeStruct((parts - 1, count, width), bf16),
        ),
        in_specs=[pl.BlockSpec(memory_space=pltpu.SMEM)] + [in_vmem()] * 4,
        out_specs=(in_vmem(), in_vmem()),
        scratch_shapes=[pltpu.VMEM((rows, width), f32)],
        compiler_params=params(8),
        cost_estimate=BRIEF,
        name="mix_rows",
    )(place, own_a, came_a, own_b, came_b)


def filter_body(h_ref, out_ref, *, order):
    dests, blocks, chans, _ = out_ref.shape
    for block in range(blocks):
        turned = h_ref[block * LANES : (block + 1) * LANES, :].astype(f32).T.astype(bf16)
        for dest in range(dests):
            first = order[dest]
            out_ref[dest, block] = turned[first : first + chans]


def filter_blocks(long_filter, order, chans):
    rows = long_filter.shape[0]
    return pl.pallas_call(
        functools.partial(filter_body, order=order),
        out_shape=jax.ShapeDtypeStruct((len(order), rows // LANES, chans, LANES), bf16),
        in_specs=[in_vmem()],
        out_specs=in_vmem(),
        compiler_params=params(32),
        cost_estimate=BRIEF,
        name="filter_blocks",
    )(long_filter)


def short_conv(padded, taps, start, size):
    total = taps[0:1] * padded[start : start + size, :]
    for lag in range(1, taps.shape[0]):
        total = total + taps[lag : lag + 1] * padded[start - lag : start - lag + size, :]
    return total


def gate_body(kept_ref, got_ref, taps_ref, out_ref, whole):
    dests, blocks, chans, _ = out_ref.shape
    half = dests * chans
    total = kept_ref[...]
    for part in range(got_ref.shape[0]):
        total = total + got_ref[part].astype(f32)
    whole[...] = total
    taps = taps_ref[...]
    for block in range(blocks):
        mixed = short_conv(whole, taps, HALO + block * LANES, LANES).T
        gated = (mixed[:half] * mixed[half:]).astype(bf16)
        for dest in range(dests):
            out_ref[dest, block] = gated[dest * chans : (dest + 1) * chans]


def gate(kept, got, taps, dests):
    rows, width = kept.shape
    blocks = (rows - HALO) // LANES
    return pl.pallas_call(
        gate_body,
        out_shape=jax.ShapeDtypeStruct((dests, blocks, width // 2 // dests, LANES), bf16),
        in_specs=[in_vmem()] * 3,
        out_specs=in_vmem(),
        scratch_shapes=[pltpu.VMEM((rows, width), f32)],
        compiler_params=params(12),
        cost_estimate=BRIEF,
        name="gate",
    )(kept, got, taps)


def conv_body(g_ref, h_ref, bias_ref, out_ref, gs, hs, *scratch, chans, blocks):
    gs[...] = g_ref[...].astype(f32)
    hs[...] = h_ref[...].astype(f32)
    row = lax.broadcasted_iota(jnp.int32, (LANES, LANES), 0)
    col = lax.broadcasted_iota(jnp.int32, (LANES, LANES), 1)
    keep = col >= row
    steps = blocks // GROUP
    sets = [scratch[i : i + 4] for i in range(0, len(scratch), 4)]
    for acc, padded, lhs, toep in sets:
        padded[0:GROUP, :] = jnp.zeros((GROUP, LANES), f32)
        padded[blocks + GROUP : blocks + 2 * GROUP, :] = jnp.zeros((GROUP, LANES), f32)

    def channels(first, _):
        every = [first + i * (chans // len(sets)) for i in range(len(sets))]
        series = []
        for c, (acc, padded, lhs, toep) in zip(every, sets):
            series.append(gs[pl.ds(c, blocks, stride=chans), :])
            padded[GROUP : GROUP + blocks, :] = series[-1]
            for r in range(GROUP):
                lhs[:, r * LANES : (r + 1) * LANES] = padded[
                    GROUP - r : GROUP - r + blocks + GROUP, :
                ].astype(bf16)
            acc[...] = jnp.zeros_like(acc)

        def build(c, step, target, before):
            for r in range(GROUP):
                taps = hs[pl.ds((step * GROUP + r) * chans + c, 1), :].astype(bf16)
                turned = pltpu.roll(
                    jnp.broadcast_to(taps, (LANES, LANES)), 0, 1, stride=1, stride_axis=0
                )
                target[r * LANES : (r + 1) * LANES, :] = jnp.where(keep, turned, before)
                before = turned
            return before

        none = jnp.zeros((LANES, LANES), bf16)
        if steps <= 8:
            before = [none] * len(sets)
            for step in range(steps):
                size = min(blocks + GROUP, blocks - step * GROUP)
                for i, (c, (acc, padded, lhs, toep)) in enumerate(zip(every, sets)):
                    target = toep.at[step % 2]
                    before[i] = build(c, step, target, before[i])
                    acc[step * GROUP : step * GROUP + size, :] += jnp.dot(
                        lhs[0:size, :], target[...], preferred_element_type=f32
                    )
        else:
            for c, (acc, padded, lhs, toep) in zip(every, sets):

                def one(step, before):
                    before = build(c, step, toep.at[0], before)
                    rows = pl.ds(pl.multiple_of(step * GROUP, GROUP), blocks + GROUP)
                    acc[rows, :] += jnp.dot(lhs[...], toep[0], preferred_element_type=f32)
                    return before

                lax.fori_loop(0, steps, one, none)
        for c, own, (acc, padded, lhs, toep) in zip(every, series, sets):
            gs[pl.ds(c, blocks, stride=chans), :] = acc[0:blocks, :] + bias_ref[0, c] * own
        return 0

    lax.fori_loop(0, chans // len(sets), channels, 0)
    out_ref[...] = gs[...].astype(bf16)


def long_conv(gated, filt, bias, chans):
    rows = gated.shape[0]
    blocks = rows // chans
    together = math.gcd(chans, 4)
    one = [
        pltpu.VMEM((2 * blocks + GROUP, LANES), f32),
        pltpu.VMEM((blocks + 2 * GROUP, LANES), f32),
        pltpu.VMEM((blocks + GROUP, GROUP * LANES), bf16),
        pltpu.VMEM((2, GROUP * LANES, LANES), bf16),
    ]
    return pl.pallas_call(
        functools.partial(conv_body, chans=chans, blocks=blocks),
        out_shape=jax.ShapeDtypeStruct((rows, LANES), bf16),
        in_specs=[in_vmem(), in_vmem(), pl.BlockSpec(memory_space=pltpu.SMEM)],
        out_specs=in_vmem(),
        scratch_shapes=[pltpu.VMEM((rows, LANES), f32), pltpu.VMEM((rows, LANES), f32)] + one * together,
        compiler_params=params(24),
        cost_estimate=BRIEF,
        name="long_conv",
    )(gated, filt, bias)


def finish_body(kept_ref, got_ref, taps_ref, z_ref, out_ref, whole, *, order):
    total = kept_ref[...]
    for part in range(got_ref.shape[0]):
        total = total + got_ref[part].astype(f32)
    whole[...] = total
    taps = taps_ref[...]
    sources = sorted(range(len(order)), key=lambda i: order[i])
    for block in range(z_ref.shape[1]):
        z = jnp.concatenate([z_ref[i, block].astype(f32) for i in sources], axis=0)
        query = short_conv(whole, taps, HALO + block * LANES, LANES)
        out_ref[block * LANES : (block + 1) * LANES, :] = (query * z.T).astype(bf16)


def finish(kept, got, taps, z, order):
    rows, width = kept.shape
    return pl.pallas_call(
        functools.partial(finish_body, order=order),
        out_shape=jax.ShapeDtypeStruct((rows - HALO, width), bf16),
        in_specs=[in_vmem()] * 4,
        out_specs=in_vmem(),
        scratch_shapes=[pltpu.VMEM((rows, width), f32)],
        compiler_params=params(32),
        cost_estimate=BRIEF,
        name="finish",
    )(kept, got, taps, z)


def swap(array, axis, by=1):
    size = lax.axis_size(axis)
    return lax.ppermute(array, axis, [(i, (i + by) % size) for i in range(size)])


def shards(tokens, w_proj, short_taps, long_filter, filter_bias):
    n_proj = lax.axis_size("proj")
    n_seq = lax.axis_size("seq")
    p = lax.axis_index("proj")
    s = lax.axis_index("seq")
    c = lax.axis_index("chan")
    rows, depth = tokens.shape
    own_rows = rows // n_proj
    channels = w_proj.shape[2]
    slab = channels // n_proj
    chans = slab // n_seq
    order = [pp * slab + ss * chans for ss in range(n_seq) for pp in range(n_proj)]

    place = jnp.stack([p, c]).astype(jnp.int32)
    barrier = lax.optimization_barrier

    def exchange(send):
        return jnp.stack([swap(send[by - 1], "proj", by) for by in range(1, n_proj)])

    w = w_proj.transpose(1, 0, 2)
    w_hbm = pltpu.with_memory_space_constraint(w, pltpu.HBM)
    other = swap(lax.dynamic_slice_in_dim(w, (1 - c) * depth, depth, 1), "chan")
    halo = lax.ppermute(tokens[rows - HALO :], "seq", [(i, i + 1) for i in range(n_seq - 1)])

    half = rows // 2
    own_a, away_a, own_qa, away_qa = project(place, tokens[:half], None, w_hbm, other, n_proj)
    came_a = swap(away_a, "chan")
    halo, away_qa = barrier((halo, away_qa))
    own_b, away_b, own_qb, away_qb = project(place, tokens[half:], halo, w_hbm, other, n_proj)
    came_b = swap(away_b, "chan")

    kept, send = mix(place, own_a, came_a, own_b, came_b)
    got = exchange(send)

    long_filter, away_qa, away_qb, send = barrier((long_filter, away_qa, away_qb, send))
    filt = filter_blocks(long_filter, order, chans)
    filt = lax.all_to_all(filt, RING, split_axis=0, concat_axis=0, tiled=True)

    kept_q, send_q = mix_rows(place, own_qa, swap(away_qa, "chan"), own_qb, swap(away_qb, "chan"), n_proj)
    got, filt, send_q = barrier((got, filt, send_q))
    got_q = exchange(send_q)

    taps_kv = lax.dynamic_slice_in_dim(short_taps[:, 1:], p * slab, slab, 2).reshape(-1, 2 * slab)
    gated = gate(kept, got, taps_kv, n_seq)
    gated = lax.all_to_all(gated, "seq", split_axis=0, concat_axis=0, tiled=True)
    gated, got_q = barrier((gated, got_q))
    bias = lax.dynamic_slice_in_dim(filter_bias, p * slab + s * chans, chans, 0)[None]
    z = long_conv(gated.reshape(-1, LANES), filt.reshape(-1, LANES), bias, chans)
    z = z.reshape(n_seq * n_proj, -1, chans, LANES)
    z = lax.all_to_all(z, RING, split_axis=0, concat_axis=0, tiled=True)
    return finish(kept_q, got_q, short_taps[:, 0], z, order)


def solution(mesh):
    placed = (
        P("seq", ("proj", "chan")),
        P("proj", None, ("groups", "chan")),
        P(None, None, ("groups", "chan")),
        P(("seq", "proj"), ("groups", "chan")),
        P(("groups", "chan")),
    )
    return jax.shard_map(
        shards,
        mesh=mesh,
        in_specs=placed,
        out_specs=P(("seq", "proj"), ("groups", "chan")),
        check_vma=False,
    )
```

```python
import functools
import math

import jax
import jax.numpy as jnp
from jax import lax
from jax.experimental import pallas as pl
from jax.experimental.pallas import tpu as pltpu
from jax.sharding import PartitionSpec as P

LANES = 128
HALO = 16
GROUP = 8
TILE = 256
BRIEF = pl.CostEstimate(flops=1, transcendentals=0, bytes_accessed=1)
f32 = jnp.float32
bf16 = jnp.bfloat16
RING = ("seq", "proj")


def in_vmem():
    return pl.BlockSpec(memory_space=pltpu.VMEM)


def params(mib):
    return pltpu.CompilerParams(vmem_limit_bytes=mib << 20)


def spread(out_ref, product, at, width):
    slabs, _, wide = out_ref.shape
    part = width // slabs
    for slab in range(slabs):
        pieces = [
            product[:, j * width + slab * part : j * width + (slab + 1) * part]
            for j in range(wide // part)
        ]
        whole = pieces[0] if len(pieces) == 1 else jnp.concatenate(pieces, axis=1)
        out_ref[slab, at : at + product.shape[0], :] = whole.astype(out_ref.dtype)


def project_body(place_ref, tok_ref, *refs, halo):
    if halo:
        halo_ref, w_ref, other_ref, kv_own, kv_away, q_own, q_away, own_w, query_w, sems = refs
    else:
        w_ref, other_ref, kv_own, kv_away, q_own, q_away, own_w, query_w, sems = refs
    rows, depth = tok_ref.shape
    width = w_ref.shape[2]
    start = place_ref[1] * depth
    targets = [(0, query_w, 0), (1, own_w, 0), (2, own_w, width)]
    copies = [
        pltpu.make_async_copy(
            w_ref.at[pick, pl.ds(start, depth), :], target.at[:, pl.ds(at, width)], sems.at[pick]
        )
        for pick, target, at in targets
    ]
    for copy in copies:
        copy.start()
    tile = min(TILE, rows)

    def passes(weights, put):
        if halo:
            put(jnp.dot(halo_ref[...], weights, preferred_element_type=f32), 0)
        for at in range(0, rows, tile):
            product = jnp.dot(tok_ref[at : at + tile, :], weights, preferred_element_type=f32)
            put(product, (HALO if halo else 0) + at)

    def put_query(product, at):
        q_own[at : at + product.shape[0], :] = product[:, :width]
        q_away[at : at + product.shape[0], :] = product[:, width:].astype(bf16)

    passes(other_ref[:, : 2 * width], lambda product, at: spread(kv_away, product, at, width))
    query_w[:, width:] = other_ref[:, 2 * width :]
    for copy in copies:
        copy.wait()
    passes(own_w[...], lambda product, at: spread(kv_own, product, at, width))
    passes(query_w[...], put_query)


def project(place, tokens, halo, w, other, slabs):
    rows, depth = tokens.shape
    width = w.shape[2]
    count = rows + (0 if halo is None else HALO)
    keys = (slabs, count, 2 * width // slabs)
    extra = [] if halo is None else [halo]
    return pl.pallas_call(
        functools.partial(project_body, halo=halo is not None),
        out_shape=(
            jax.ShapeDtypeStruct(keys, f32),
            jax.ShapeDtypeStruct(keys, bf16),
            jax.ShapeDtypeStruct((count, width), f32),
            jax.ShapeDtypeStruct((count, width), bf16),
        ),
        in_specs=[pl.BlockSpec(memory_space=pltpu.SMEM)]
        + [in_vmem()] * (1 + len(extra))
        + [pl.BlockSpec(memory_space=pl.ANY), in_vmem()],
        out_specs=(in_vmem(),) * 4,
        scratch_shapes=[
            pltpu.VMEM((depth, 2 * width), bf16),
            pltpu.VMEM((depth, 2 * width), bf16),
            pltpu.SemaphoreType.DMA((3,)),
        ],
        compiler_params=params(14),
        cost_estimate=BRIEF,
        name="project",
    )(place, tokens, *extra, w, other)


def mix_body(place_ref, own_a, came_a, own_b, came_b, kept_ref, send_ref):
    slabs, rows = own_a.shape[:2]
    p = place_ref[0]

    def put(slab, store):
        last = own_b[slab] + came_b[slab].astype(f32)
        store(pl.ds(0, HALO), last[:HALO])
        store(pl.ds(HALO, rows), own_a[slab] + came_a[slab].astype(f32))
        store(pl.ds(HALO + rows, last.shape[0] - HALO), last[HALO:])

    def keep(at, value):
        kept_ref[at, :] = value

    put(p, keep)
    for by in range(1, slabs):

        def send(at, value):
            send_ref[by - 1, at, :] = value.astype(bf16)

        put(lax.rem(p + by, slabs), send)


def mix(place, own_a, came_a, own_b, came_b):
    slabs, rows, width = own_a.shape
    rows += own_b.shape[1]
    return pl.pallas_call(
        mix_body,
        out_shape=(
            jax.ShapeDtypeStruct((rows, width), f32),
            jax.ShapeDtypeStruct((slabs - 1, rows, width), bf16),
        ),
        in_specs=[pl.BlockSpec(memory_space=pltpu.SMEM)] + [in_vmem()] * 4,
        out_specs=(in_vmem(), in_vmem()),
        compiler_params=params(8),
        cost_estimate=BRIEF,
        name="mix",
    )(place, own_a, came_a, own_b, came_b)


def mix_rows_body(place_ref, own_a, came_a, own_b, came_b, kept_ref, send_ref, whole):
    parts = send_ref.shape[0] + 1
    count = kept_ref.shape[0]
    step = count - HALO
    rows = own_a.shape[0]
    p = place_ref[0]
    last = own_b[...] + came_b[...].astype(f32)
    whole[0:HALO, :] = last[:HALO]
    whole[HALO : HALO + rows, :] = own_a[...] + came_a[...].astype(f32)
    whole[HALO + rows :, :] = last[HALO:]

    def part(i):
        return whole[pl.ds(pl.multiple_of(i * step, HALO), count), :]

    kept_ref[...] = part(p)
    for by in range(1, parts):
        send_ref[by - 1] = part(lax.rem(p + by, parts)).astype(bf16)


def mix_rows(place, own_a, came_a, own_b, came_b, parts):
    rows, width = own_a.shape
    rows += own_b.shape[0]
    count = (rows - HALO) // parts + HALO
    return pl.pallas_call(
        mix_rows_body,
        out_shape=(
            jax.ShapeDtypeStruct((count, width), f32),
            jax.ShapeDtypeStruct((parts - 1, count, width), bf16),
        ),
        in_specs=[pl.BlockSpec(memory_space=pltpu.SMEM)] + [in_vmem()] * 4,
        out_specs=(in_vmem(), in_vmem()),
        scratch_shapes=[pltpu.VMEM((rows, width), f32)],
        compiler_params=params(8),
        cost_estimate=BRIEF,
        name="mix_rows",
    )(place, own_a, came_a, own_b, came_b)


def filter_body(h_ref, out_ref, *, order):
    dests, blocks, chans, _ = out_ref.shape
    for block in range(blocks):
        turned = h_ref[block * LANES : (block + 1) * LANES, :].astype(f32).T.astype(bf16)
        for dest in range(dests):
            first = order[dest]
            out_ref[dest, block] = turned[first : first + chans]


def filter_blocks(long_filter, order, chans):
    rows = long_filter.shape[0]
    return pl.pallas_call(
        functools.partial(filter_body, order=order),
        out_shape=jax.ShapeDtypeStruct((len(order), rows // LANES, chans, LANES), bf16),
        in_specs=[in_vmem()],
        out_specs=in_vmem(),
        compiler_params=params(32),
        cost_estimate=BRIEF,
        name="filter_blocks",
    )(long_filter)


def short_conv(padded, taps, start, size):
    total = taps[0:1] * padded[start : start + size, :]
    for lag in range(1, taps.shape[0]):
        total = total + taps[lag : lag + 1] * padded[start - lag : start - lag + size, :]
    return total


def gate_body(kept_ref, got_ref, taps_ref, out_ref, whole):
    dests, blocks, chans, _ = out_ref.shape
    half = dests * chans
    total = kept_ref[...]
    for part in range(got_ref.shape[0]):
        total = total + got_ref[part].astype(f32)
    whole[...] = total
    taps = taps_ref[...]
    for block in range(blocks):
        mixed = short_conv(whole, taps, HALO + block * LANES, LANES).T
        gated = (mixed[:half] * mixed[half:]).astype(bf16)
        for dest in range(dests):
            out_ref[dest, block] = gated[dest * chans : (dest + 1) * chans]


def gate(kept, got, taps, dests):
    rows, width = kept.shape
    blocks = (rows - HALO) // LANES
    return pl.pallas_call(
        gate_body,
        out_shape=jax.ShapeDtypeStruct((dests, blocks, width // 2 // dests, LANES), bf16),
        in_specs=[in_vmem()] * 3,
        out_specs=in_vmem(),
        scratch_shapes=[pltpu.VMEM((rows, width), f32)],
        compiler_params=params(12),
        cost_estimate=BRIEF,
        name="gate",
    )(kept, got, taps)


def conv_body(g_ref, h_ref, bias_ref, out_ref, gs, hs, *scratch, chans, blocks):
    gs[...] = g_ref[...].astype(f32)
    hs[...] = h_ref[...].astype(f32)
    row = lax.broadcasted_iota(jnp.int32, (LANES, LANES), 0)
    col = lax.broadcasted_iota(jnp.int32, (LANES, LANES), 1)
    keep = col >= row
    steps = blocks // GROUP
    sets = [scratch[i : i + 4] for i in range(0, len(scratch), 4)]
    for acc, padded, lhs, toep in sets:
        padded[0:GROUP, :] = jnp.zeros((GROUP, LANES), f32)
        padded[blocks + GROUP : blocks + 2 * GROUP, :] = jnp.zeros((GROUP, LANES), f32)

    def channels(first, _):
        every = [first + i * (chans // len(sets)) for i in range(len(sets))]
        series = []
        for c, (acc, padded, lhs, toep) in zip(every, sets):
            series.append(gs[pl.ds(c, blocks, stride=chans), :])
            padded[GROUP : GROUP + blocks, :] = series[-1]
            for r in range(GROUP):
                lhs[:, r * LANES : (r + 1) * LANES] = padded[
                    GROUP - r : GROUP - r + blocks + GROUP, :
                ].astype(bf16)
            acc[...] = jnp.zeros_like(acc)

        def build(c, step, target, before):
            for r in range(GROUP):
                taps = hs[pl.ds((step * GROUP + r) * chans + c, 1), :].astype(bf16)
                turned = pltpu.roll(
                    jnp.broadcast_to(taps, (LANES, LANES)), 0, 1, stride=1, stride_axis=0
                )
                target[r * LANES : (r + 1) * LANES, :] = jnp.where(keep, turned, before)
                before = turned
            return before

        none = jnp.zeros((LANES, LANES), bf16)
        if steps <= 8:
            before = [none] * len(sets)
            for step in range(steps):
                size = min(blocks + GROUP, blocks - step * GROUP)
                for i, (c, (acc, padded, lhs, toep)) in enumerate(zip(every, sets)):
                    target = toep.at[step % 2]
                    before[i] = build(c, step, target, before[i])
                    acc[step * GROUP : step * GROUP + size, :] += jnp.dot(
                        lhs[0:size, :], target[...], preferred_element_type=f32
                    )
        else:
            for c, (acc, padded, lhs, toep) in zip(every, sets):

                def one(step, before):
                    before = build(c, step, toep.at[0], before)
                    rows = pl.ds(pl.multiple_of(step * GROUP, GROUP), blocks + GROUP)
                    acc[rows, :] += jnp.dot(lhs[...], toep[0], preferred_element_type=f32)
                    return before

                lax.fori_loop(0, steps, one, none)
        for c, own, (acc, padded, lhs, toep) in zip(every, series, sets):
            gs[pl.ds(c, blocks, stride=chans), :] = acc[0:blocks, :] + bias_ref[0, c] * own
        return 0

    lax.fori_loop(0, chans // len(sets), channels, 0)
    out_ref[...] = gs[...].astype(bf16)


def long_conv(gated, filt, bias, chans):
    rows = gated.shape[0]
    blocks = rows // chans
    together = math.gcd(chans, 8)
    one = [
        pltpu.VMEM((2 * blocks + GROUP, LANES), f32),
        pltpu.VMEM((blocks + 2 * GROUP, LANES), f32),
        pltpu.VMEM((blocks + GROUP, GROUP * LANES), bf16),
        pltpu.VMEM((2, GROUP * LANES, LANES), bf16),
    ]
    return pl.pallas_call(
        functools.partial(conv_body, chans=chans, blocks=blocks),
        out_shape=jax.ShapeDtypeStruct((rows, LANES), bf16),
        in_specs=[in_vmem(), in_vmem(), pl.BlockSpec(memory_space=pltpu.SMEM)],
        out_specs=in_vmem(),
        scratch_shapes=[pltpu.VMEM((rows, LANES), f32), pltpu.VMEM((rows, LANES), f32)] + one * together,
        compiler_params=params(24),
        cost_estimate=BRIEF,
        name="long_conv",
    )(gated, filt, bias)


def finish_body(kept_ref, got_ref, taps_ref, z_ref, out_ref, whole, *, order):
    total = kept_ref[...]
    for part in range(got_ref.shape[0]):
        total = total + got_ref[part].astype(f32)
    whole[...] = total
    taps = taps_ref[...]
    sources = sorted(range(len(order)), key=lambda i: order[i])
    for block in range(z_ref.shape[1]):
        z = jnp.concatenate([z_ref[i, block].astype(f32) for i in sources], axis=0)
        query = short_conv(whole, taps, HALO + block * LANES, LANES)
        out_ref[block * LANES : (block + 1) * LANES, :] = (query * z.T).astype(bf16)


def finish(kept, got, taps, z, order):
    rows, width = kept.shape
    return pl.pallas_call(
        functools.partial(finish_body, order=order),
        out_shape=jax.ShapeDtypeStruct((rows - HALO, width), bf16),
        in_specs=[in_vmem()] * 4,
        out_specs=in_vmem(),
        scratch_shapes=[pltpu.VMEM((rows, width), f32)],
        compiler_params=params(32),
        cost_estimate=BRIEF,
        name="finish",
    )(kept, got, taps, z)


def swap(array, axis, by=1):
    size = lax.axis_size(axis)
    return lax.ppermute(array, axis, [(i, (i + by) % size) for i in range(size)])


def shards(tokens, w_proj, short_taps, long_filter, filter_bias):
    n_proj = lax.axis_size("proj")
    n_seq = lax.axis_size("seq")
    p = lax.axis_index("proj")
    s = lax.axis_index("seq")
    c = lax.axis_index("chan")
    rows, depth = tokens.shape
    own_rows = rows // n_proj
    channels = w_proj.shape[2]
    slab = channels // n_proj
    chans = slab // n_seq
    order = [pp * slab + ss * chans for ss in range(n_seq) for pp in range(n_proj)]

    place = jnp.stack([p, c]).astype(jnp.int32)
    barrier = lax.optimization_barrier

    def exchange(send):
        return jnp.stack([swap(send[by - 1], "proj", by) for by in range(1, n_proj)])

    w = w_proj.transpose(1, 0, 2)
    w_hbm = pltpu.with_memory_space_constraint(w, pltpu.HBM)
    theirs = [
        lax.dynamic_slice(w, (pick, (1 - c) * depth, 0), (1, depth, channels))[0]
        for pick in (1, 2, 0)
    ]
    other = swap(jnp.concatenate(theirs, axis=1), "chan")
    halo = lax.ppermute(tokens[rows - HALO :], "seq", [(i, i + 1) for i in range(n_seq - 1)])

    half = rows // 2
    own_a, away_a, own_qa, away_qa = project(place, tokens[:half], None, w_hbm, other, n_proj)
    came_a = swap(away_a, "chan")
    halo, away_qa = barrier((halo, away_qa))
    own_b, away_b, own_qb, away_qb = project(place, tokens[half:], halo, w_hbm, other, n_proj)
    came_b = swap(away_b, "chan")

    kept, send = mix(place, own_a, came_a, own_b, came_b)
    got = exchange(send)

    long_filter, away_qa, away_qb, send = barrier((long_filter, away_qa, away_qb, send))
    filt = filter_blocks(long_filter, order, chans)
    filt = lax.all_to_all(filt, RING, split_axis=0, concat_axis=0, tiled=True)

    kept_q, send_q = mix_rows(place, own_qa, swap(away_qa, "chan"), own_qb, swap(away_qb, "chan"), n_proj)
    got, filt, send_q = barrier((got, filt, send_q))
    got_q = exchange(send_q)

    taps_kv = lax.dynamic_slice_in_dim(short_taps[:, 1:], p * slab, slab, 2).reshape(-1, 2 * slab)
    gated = gate(kept, got, taps_kv, n_seq)
    gated = lax.all_to_all(gated, "seq", split_axis=0, concat_axis=0, tiled=True)
    gated, got_q = barrier((gated, got_q))
    bias = lax.dynamic_slice_in_dim(filter_bias, p * slab + s * chans, chans, 0)[None]
    z = long_conv(gated.reshape(-1, LANES), filt.reshape(-1, LANES), bias, chans)
    z = z.reshape(n_seq * n_proj, -1, chans, LANES)
    z = lax.all_to_all(z, RING, split_axis=0, concat_axis=0, tiled=True)
    return finish(kept_q, got_q, short_taps[:, 0], z, order)


def solution(mesh):
    placed = (
        P("seq", ("proj", "chan")),
        P("proj", None, ("groups", "chan")),
        P(None, None, ("groups", "chan")),
        P(("seq", "proj"), ("groups", "chan")),
        P(("groups", "chan")),
    )
    return jax.shard_map(
        shards,
        mesh=mesh,
        in_specs=placed,
        out_specs=P(("seq", "proj"), ("groups", "chan")),
        check_vma=False,
    )
```
